32 devices in a mesh: tiles: 8 (over z, x), lev: 4 (over y, core).
Axes of the slice: x: 2, y: 2, z: 4, core: 2. Of those that a mesh axis runs over, the one named last changes fastest.
Arguments:
- land_smb: bfloat16 [512, 10, 128], P(('tiles', 'lev')), may hold values from -6 to 6
- block_weights: bfloat16 [1024, 128, 1024], P(('tiles', 'lev')), may hold values from -0.5 to 0.5
- block_tile: int32 [1024], P(('tiles', 'lev')), may hold values from 0 to 255, as said below
- block_land: int32 [1024], P(('tiles', 'lev')), may hold values from 0 to 15
- block_class: int32 [1024], P(('tiles', 'lev')), may hold values from 0 to 9
- ice_mask: int32 [64, 4096], P('tiles', 'lev'), may hold values 0 or 1
- thickness: float32 [64, 4096], P('tiles', 'lev'), may hold values from 0.5 to 2
- prev_smb: float32 [64, 4096], P('tiles', 'lev'), may hold values from -6 to 6
- basal_friction: float32 [64, 4096], P('tiles', 'lev'), may hold values from 0.05 to 0.5
- driving: float32 [10, 64, 4096], P(None, 'tiles', 'lev'), may hold values from -54 to 54
- velocity_start: float32 [10, 64, 4096], P(None, 'tiles', 'lev'), may hold values from -6 to 6
Outputs:
- ice_smb: float32 [64, 4096], P('tiles')
- velocity_end: float32 [10, 64, 4096], P(None, 'tiles', 'lev')
The draws below stay inside these ranges and needn't reach their ends.
Inputs may be any that keep to these rules, and one draw needn't show every extreme that they name: `block_tile`: ice tile t lies on index t // 32 of tiles. Of the 32 remap blocks of one device, at most 8 name tiles on any one index of tiles; in every draw some index of tiles receives exactly 8 from every device.
All inputs are finite; a program needn't handle non-finite values. No bound on the sum of `ice_mask` on one device may be relied on, other than what follows from the above.
Results may differ from the reference program's by a relative error of at most 0.0003.
Values sent between devices are 32-bit elements; how exact they have to be, the bound alone decides.
A program may use at most 64 MiB of HBM per device.

```python
import math
import jax
import jax.numpy as jnp
from jax import lax

CX = 8
TW = 128
TPD = 32
LEVELS = 10
EC = 10
LC = 128
LAND_DEV = 16
BLK_DEV = 32
ITERS = 4
PICARD = 1
NX = 64
NY = 4096
TILE = 1024
TILES_ALL = 256
LAND_BLOCKS = 512
BLOCKS = 1024
CAP = 8
N_TILES = 8


def draw_block_tile(key, part):
    sources = BLOCKS // BLK_DEV
    owners = TILES_ALL // TPD
    others = (owners - 1) * CAP
    base = jax.random.fold_in(key, 11)
    key_hot, key_perm, key_local, key_order = jax.random.split(base, 4)
    hot_owner = jax.random.randint(key_hot, (), 0, owners)

    def one_source(pair_keys):
        chosen = jax.random.permutation(pair_keys[0], others)[:BLK_DEV - CAP]
        target = (chosen // CAP).astype(jnp.int32)
        target = target + (target >= hot_owner).astype(jnp.int32)
        merged = jnp.concatenate([jnp.full((CAP,), 0, jnp.int32) + hot_owner.astype(jnp.int32), target])
        return jax.random.permutation(pair_keys[1], merged)
    keys_one = jax.random.split(key_perm, sources)
    keys_two = jax.random.split(key_order, sources)
    targets = jax.vmap(one_source)(jnp.stack([keys_one, keys_two], axis=1))
    local = jax.random.randint(key_local, (sources, BLK_DEV), 0, TPD)
    return (targets * TPD + local).astype(jnp.int32).reshape(BLOCKS)


def draw_driving(key, part):
    base = jax.random.fold_in(key, 23)
    key_main = jax.random.fold_in(base, 0)
    level_pos = jnp.arange(LEVELS, dtype=jnp.float32) / max(LEVELS - 1, 1)
    row_pos = jnp.arange(NX, dtype=jnp.float32) / NX
    scales = (1.0 + 2.0 * level_pos)[:, None, None] * (1.0 + 2.0 * row_pos)[None, :, None]
    values = jnp.clip(jax.random.normal(key_main, (LEVELS, NX, NY), jnp.float32), -6.0, 6.0)
    return values * scales


def set_ends(entries, rng, smallest, top_value):
    extent = entries.shape
    place = [jax.random.randint(jax.random.fold_in(rng, axis), (), 0, extent[axis]) for axis in range(len(extent))]
    entries = entries.at[tuple(place)].set(smallest)
    longest = extent.index(max(extent))
    place[longest] = (place[longest] + 1) % extent[longest]
    return entries.at[tuple(place)].set(top_value)


def steps_of(stream_key, extent, cuts, low, top_value):
    gain = 1.0
    for dim, blocks in cuts:
        steps = jax.random.uniform(jax.random.fold_in(jax.random.fold_in(stream_key, 6), dim), (blocks,), jnp.float32, low / len(cuts), top_value / len(cuts))
        gain = gain * jnp.repeat(jnp.exp(steps), extent[dim] // blocks).reshape((-1,) + (1,) * (len(extent) - 1 - dim))
    return gain


def gaussian(key, extent, scale, limit, cuts=(), kind=jnp.bfloat16):
    values = jax.random.normal(key, extent, jnp.float32) * scale
    if len(cuts) > 0:
        values = steps_of(key, extent, cuts, -0.22, 0.18) * values
    return jnp.clip(values, min=-limit, max=limit).astype(kind)


def setup_inputs(seed: int = 0) -> dict:
    key_of = jax.random.split(jax.random.key(seed), 12)
    land_smb = gaussian(key_of[0], (LAND_BLOCKS, EC, LC), 1.0, 6.0, ((0, 32),))
    block_weights = gaussian(key_of[1], (BLOCKS, LC, TILE), LC ** -0.5, 0.5, ((0, 32),))
    block_tile = draw_block_tile(jax.random.fold_in(key_of[11], 71), 0)
    block_land = set_ends(jax.random.randint(key_of[3], (BLOCKS,), 0, LAND_DEV), jax.random.fold_in(key_of[3], 1), 0, LAND_DEV - 1).astype(jnp.int32)
    block_class = set_ends(jax.random.randint(key_of[4], (BLOCKS,), 0, EC), jax.random.fold_in(key_of[4], 1), 0, EC - 1).astype(jnp.int32)
    ice_mask = set_ends((jax.random.randint(key_of[5], (NX, NY), 0, 4) < 3).astype(jnp.int32), jax.random.fold_in(key_of[5], 1), 0, 1)
    thickness = jnp.clip(jnp.exp(math.log(2.0) - 1.3862944 * jax.random.uniform(key_of[6], (NX, NY), jnp.float32) ** steps_of(key_of[6], (NX, NY), ((0, 8), (1, 4)), -0.2, 0.2)), 0.5, 2.0)
    prev_smb = gaussian(key_of[7], (NX, NY), 1.0, 6.0, ((0, 8), (1, 4)), jnp.float32)
    basal_friction = jnp.clip(jnp.exp(math.log(0.5) - 2.3025851 * jax.random.uniform(key_of[8], (NX, NY), jnp.float32) ** steps_of(key_of[8], (NX, NY), ((0, 8), (1, 4)), -0.2, 0.2)), 0.05, 0.5)
    driving = draw_driving(jax.random.fold_in(key_of[11], 71), 0)
    velocity_start = gaussian(key_of[10], (LEVELS, NX, NY), 1.0, 6.0, ((1, 8), (2, 4)), jnp.float32)
    return {"land_smb": land_smb, "block_weights": block_weights, "block_tile": block_tile, "block_land": block_land, "block_class": block_class, "ice_mask": ice_mask, "thickness": thickness, "prev_smb": prev_smb, "basal_friction": basal_friction, "driving": driving, "velocity_start": velocity_start}


VISC_FLOOR = 0.25
VERTICAL = 4.0
SMB_WEIGHT = 0.5

def visc_from(box, ice_frac):
    slope_x = (box[:, 2:, 1:-1] - box[:, :-2, 1:-1]) * 0.5
    slope_y = (box[:, 1:-1, 2:] - box[:, 1:-1, :-2]) * 0.5
    return ice_frac * (VISC_FLOOR + slope_x * slope_x + slope_y * slope_y) ** (-1.0 / 3.0)

def face_weights(visc_box, drag):
    center = visc_box[1:-1, 1:-1, 1:-1]
    east_face = jnp.sqrt(center * visc_box[1:-1, 2:, 1:-1])
    west_face = jnp.sqrt(center * visc_box[1:-1, :-2, 1:-1])
    north_face = jnp.sqrt(center * visc_box[1:-1, 1:-1, 2:])
    south_face = jnp.sqrt(center * visc_box[1:-1, 1:-1, :-2])
    upper_face = VERTICAL * jnp.sqrt(center * visc_box[2:, 1:-1, 1:-1])
    lower_face = VERTICAL * jnp.sqrt(center * visc_box[:-2, 1:-1, 1:-1])
    diagonal_sum = drag + east_face + west_face + north_face + south_face + upper_face + lower_face
    return (diagonal_sum, east_face, west_face, upper_face, lower_face, north_face, south_face)

def apply_operator(faces, field_box):
    diagonal_sum, east_face, west_face, upper_face, lower_face, north_face, south_face = faces
    center = field_box[1:-1, 1:-1, 1:-1]
    result = diagonal_sum * center - east_face * field_box[1:-1, 2:, 1:-1] - west_face * field_box[1:-1, :-2, 1:-1]
    result = result - upper_face * field_box[2:, 1:-1, 1:-1] - lower_face * field_box[:-2, 1:-1, 1:-1]
    return result - north_face * field_box[1:-1, 1:-1, 2:] - south_face * field_box[1:-1, 1:-1, :-2]

def padded_box(field):
    return jnp.pad(field, 1)

def krylov(faces, rhs, start):
    solution = start
    residual = rhs - apply_operator(faces, padded_box(start))
    direction = residual
    norm_now = jnp.sum(residual * residual)
    for iteration in range(ITERS):
        image = apply_operator(faces, padded_box(direction))
        step_len = norm_now / jnp.sum(direction * image)
        solution = solution + step_len * direction
        residual = residual - step_len * image
        norm_next = jnp.sum(residual * residual)
        direction = residual + norm_next / norm_now * direction
        norm_now = norm_next
    return solution

def reference(land_smb, block_weights, block_tile, block_land, block_class, ice_mask, thickness, prev_smb, basal_friction, driving, velocity_start):
    land_rows = land_smb.reshape(-1, LC)
    owners_all = BLOCKS // BLK_DEV
    source = jnp.arange(BLOCKS, dtype=jnp.int32) // BLK_DEV * LAND_DEV + block_land
    picked = land_rows[(source * EC + block_class).astype(jnp.int32)]

    def accumulate(totals, inputs):
        picked_rows, weight_rows, tiles_here = inputs
        product = jnp.einsum('bl,blt->bt', picked_rows.astype(jnp.float32), weight_rows.astype(jnp.float32), precision=lax.Precision.HIGHEST)
        return (totals + jax.ops.segment_sum(product, tiles_here, num_segments=TILES_ALL), None)
    totals, _ = lax.scan(accumulate, jnp.zeros((TILES_ALL, TILE), jnp.float32), (picked.reshape(owners_all, BLK_DEV, LC), block_weights.reshape(owners_all, BLK_DEV, LC, TILE), block_tile.reshape(owners_all, BLK_DEV)))
    ice_smb = totals.reshape(N_TILES, TPD, CX, TW).transpose(0, 2, 1, 3).reshape(NX, NY)
    ice_frac = ice_mask.astype(jnp.float32)
    rhs = (ice_frac * (thickness + SMB_WEIGHT * prev_smb))[None] * driving
    drag = (ice_frac * basal_friction + (1.0 - ice_frac))[None]
    velocity = velocity_start
    for picard_turn in range(PICARD):
        x_box = jnp.pad(velocity, ((0, 0), (1, 1), (1, 1)))
        viscosity = visc_from(x_box, ice_frac[None])
        faces = face_weights(padded_box(viscosity), drag)
        velocity = krylov(faces, rhs, velocity)
    return (ice_smb, velocity)
```

```python
import functools

import jax
import jax.numpy as jnp
from jax import lax
from jax.experimental import pallas as pl
from jax.experimental.pallas import tpu as pltpu
from jax.sharding import PartitionSpec as P

ITERS = 4
VISC_FLOOR = 0.25
VERTICAL = 4.0
SMB_WEIGHT = 0.5
SIGMA = 10.0
LANES = 128
MESH = pl.DeviceIdType.MESH
F32 = jnp.float32


def kernel(
    T, Q, cap, tpd,
    land, wts, btile, bland, bclass, mask, thk, prev, fric, drv, vel,
    tot_out, vel_out,
    v_e, drv_e, thk_e, prev_e, fric_e, mask_e,
    s_f, d_f, w_f, k_f,
    vsu, vsd, vrt, vrb, su, sd, rt, rb, sht, shb,
    dots, g_send, g_lev, g_mid, g_til,
    wbuf, lbuf, idx_m, tile_m, payload, rec, part, rs_rec, tot_s,
    loc_sem, w_sem, col_ss, col_rs, row_ss, row_rs, v_ss, v_rs,
    gl_ss, gl_rs, gt_ss, gt_rs, a_ss, a_rs, r_ss, r_rs, t_ss, t_rs,
):
    mt = lax.axis_index("tiles")
    ml = lax.axis_index("lev")
    levels, rows, cols = vel.shape
    wide = cols + 2 * LANES
    nblk = wts.shape[0]
    cells = wts.shape[2]
    inv_sigma = 1.0 / SIGMA

    def remote(src, dst, ss, rs, **where):
        return pltpu.make_async_remote_copy(
            src_ref=src, dst_ref=dst, send_sem=ss, recv_sem=rs,
            device_id=where, device_id_type=MESH)

    raw = (vel, drv, thk, prev, fric, mask)
    ext = (v_e, drv_e, thk_e, prev_e, fric_e, mask_e)

    def mid(ref):
        return ref.at[..., pl.ds(LANES, cols)]

    for k in range(6):
        pltpu.make_async_copy(raw[k], mid(ext[k]), loc_sem.at[k]).start()
    nchunk = w_sem.shape[0]
    per = nblk // nchunk
    for c in range(nchunk):
        pltpu.make_async_copy(wts.at[pl.ds(c * per, per)], wbuf.at[pl.ds(c * per, per)], w_sem.at[c]).start()

    bar = pltpu.get_barrier_semaphore()
    for d in range(1, Q):
        pl.semaphore_signal(bar, inc=1, device_id={"lev": lax.rem(ml + d, Q)}, device_id_type=MESH)
    for d in range(1, T):
        pl.semaphore_signal(bar, inc=1, device_id={"tiles": lax.rem(mt + d, T)}, device_id_type=MESH)

    s_f[0] = jnp.zeros((rows, wide), F32)
    s_f[levels + 1] = jnp.zeros((rows, wide), F32)
    w_f[0] = jnp.zeros((rows, wide), F32)
    w_f[levels + 1] = jnp.zeros((rows, wide), F32)

    @pl.when(mt == 0)
    def _():
        vrt[...] = jnp.zeros(vrt.shape, F32)
        rt[...] = jnp.zeros(rt.shape, F32)

    @pl.when(mt == T - 1)
    def _():
        vrb[...] = jnp.zeros(vrb.shape, F32)
        rb[...] = jnp.zeros(rb.shape, F32)

    for ref in ext:
        @pl.when(ml == 0)
        def _():
            ref[..., 0:LANES] = jnp.zeros(ref.shape[:-1] + (LANES,), ref.dtype)

        @pl.when(ml == Q - 1)
        def _():
            ref[..., LANES + cols:] = jnp.zeros(ref.shape[:-1] + (LANES,), ref.dtype)

    pl.semaphore_wait(bar, Q - 1 + T - 1)

    def col_right(k):
        return remote(raw[k].at[..., pl.ds(cols - LANES, LANES)], ext[k].at[..., pl.ds(0, LANES)],
                      col_ss.at[k, 0], col_rs.at[k, 0], lev=ml + 1)

    def col_left(k):
        return remote(raw[k].at[..., pl.ds(0, LANES)], ext[k].at[..., pl.ds(LANES + cols, LANES)],
                      col_ss.at[k, 1], col_rs.at[k, 1], lev=ml - 1)

    @pl.when(ml < Q - 1)
    def _():
        for k in (0, 5, 1, 2, 3, 4):
            col_right(k).start()

    @pl.when(ml > 0)
    def _():
        for k in (0, 5, 1, 2, 3, 4):
            col_left(k).start()

    def col_wait(ks):
        for k in ks:
            pltpu.make_async_copy(raw[k], mid(ext[k]), loc_sem.at[k]).wait()

        @pl.when(ml > 0)
        def _():
            for k in ks:
                col_right(k).wait_recv()

        @pl.when(ml < Q - 1)
        def _():
            for k in ks:
                col_left(k).wait_recv()

    classes = land.shape[1]
    stride = lbuf.shape[0] // land.shape[0]
    lbuf[...] = jnp.zeros(lbuf.shape, lbuf.dtype)
    for i in range(land.shape[0]):
        lbuf[stride * i:stride * i + classes, :] = land[i].astype(F32)
    for b in range(nblk):
        idx_m[b:b + 1, :] = jnp.full((1, idx_m.shape[1]), bland[b] * stride + bclass[b], jnp.int32)
        tile_m[b:b + 1, :] = jnp.full((1, LANES), btile[b], jnp.int32)
    pick_hot = (idx_m[...] == lax.broadcasted_iota(jnp.int32, idx_m.shape, 1)).astype(jnp.bfloat16)
    picked = jnp.dot(pick_hot, lbuf[...].astype(jnp.bfloat16), preferred_element_type=F32)
    tiles_b = tile_m[...]
    dest = tiles_b // tpd
    sub = lax.broadcasted_iota(jnp.int32, (nblk, LANES), 0)
    lane = lax.broadcasted_iota(jnp.int32, (nblk, LANES), 1)
    dest_row = jnp.sum(jnp.where(sub == lane, dest, 0), axis=0, keepdims=True)
    rank = jnp.sum(jnp.where(jnp.logical_and(dest == dest_row, lane < sub), 1.0, 0.0), axis=1, keepdims=True)
    slot = dest * cap + rank.astype(jnp.int32)
    local_id = (tiles_b % tpd + 1).astype(F32)
    nslot = T * cap
    slot_iota = lax.broadcasted_iota(jnp.int32, (nslot, LANES), 0)
    ids = jnp.zeros((nslot, LANES), F32)
    lhs = []
    for b in range(nblk):
        hit = slot_iota == slot[b:b + 1, :]
        ids = ids + jnp.where(hit, local_id[b:b + 1, :], 0.0)
        lhs.append(jnp.where(hit, picked[b:b + 1, :], 0.0).astype(jnp.bfloat16))

    col_wait((0, 5))
    for l in range(levels):
        x = v_e[l]
        vsu[l:l + 1, :] = x[0:1, :]
        vsu[levels + l:levels + l + 1, :] = x[1:2, :]
        vsd[l:l + 1, :] = x[rows - 1:rows, :]
        vsd[levels + l:levels + l + 1, :] = x[rows - 2:rows - 1, :]
    frac = mask_e[...].astype(F32)
    vsu[2 * levels:2 * levels + 1, :] = frac[0:1, :]
    vsd[2 * levels:2 * levels + 1, :] = frac[rows - 1:rows, :]

    def v_up():
        return remote(vsu, vrb, v_ss.at[0], v_rs.at[0], tiles=mt - 1)

    def v_down():
        return remote(vsd, vrt, v_ss.at[1], v_rs.at[1], tiles=mt + 1)

    @pl.when(mt > 0)
    def _():
        v_up().start()

    @pl.when(mt < T - 1)
    def _():
        v_down().start()

    acc = jnp.zeros((nslot, cells), F32)
    for c in range(nchunk):
        pltpu.make_async_copy(wts.at[pl.ds(c * per, per)], wbuf.at[pl.ds(c * per, per)], w_sem.at[c]).wait()
        left = jnp.concatenate(lhs[c * per:(c + 1) * per], axis=1)
        right = wbuf[c * per:(c + 1) * per].reshape(per * LANES, cells)
        acc = acc + jnp.dot(left, right, preferred_element_type=F32)
    for t in range(T):
        payload[t, :, 0:cells] = acc[t * cap:(t + 1) * cap, :]
        payload[t, :, cells:] = ids[t * cap:(t + 1) * cap, :]

    col_wait((1, 2, 3, 4))

    @pl.when(mt < T - 1)
    def _():
        v_up().wait_recv()

    @pl.when(mt > 0)
    def _():
        v_down().wait_recv()

    def a2a(d):
        to = lax.rem(mt + d, T)
        return remote(payload.at[to], rec.at[d - 1], a_ss.at[d - 1], a_rs.at[d - 1], tiles=to)

    for d in range(1, T):
        a2a(d).start()

    row_id = lax.broadcasted_iota(jnp.int32, (rows, wide), 0)

    def around(x, top, bot):
        after = jnp.where(row_id == rows - 1, bot, pltpu.roll(x, rows - 1, 0))
        before = jnp.where(row_id == 0, top, pltpu.roll(x, 1, 0))
        return before, after, pltpu.roll(x, 1, 1), pltpu.roll(x, wide - 1, 1)

    root = SIGMA ** -0.5

    def s_from(dx, dy, fr):
        q = VISC_FLOOR + 0.25 * (dx * dx) + 0.25 * (dy * dy)
        return fr * (root * jnp.exp(jnp.log(q) * (-1.0 / 6.0)))

    near_t, far_t = vrt[0:levels, :], vrt[levels:2 * levels, :]
    near_b, far_b = vrb[0:levels, :], vrb[levels:2 * levels, :]
    own_t, own_b = vsu[0:levels, :], vsd[0:levels, :]
    sht[...] = s_from(own_t - far_t, pltpu.roll(near_t, wide - 1, 1) - pltpu.roll(near_t, 1, 1),
                      vrt[2 * levels:2 * levels + 1, :])
    shb[...] = s_from(far_b - own_b, pltpu.roll(near_b, wide - 1, 1) - pltpu.roll(near_b, 1, 1),
                      vrb[2 * levels:2 * levels + 1, :])

    def s_level(l, carry):
        x = v_e[l]
        before, after, low, high = around(x, vrt[pl.ds(l, 1), :], vrb[pl.ds(l, 1), :])
        s = s_from(after - before, high - low, frac)
        s_f[l + 1] = s
        w_f[l + 1] = s * x
        return carry

    lax.fori_loop(0, levels, s_level, 0)

    def total(ref, l, top, bot):
        before, after, low, high = around(ref[l + 1], top, bot)
        return ((before + after) + (low + high)) + VERTICAL * (ref[l] + ref[l + 2])

    drag = frac * fric_e[...] + (1.0 - frac)
    drag_s = drag * inv_sigma - 1.0
    coef = frac * (thk_e[...] + SMB_WEIGHT * prev_e[...])

    def start_level(l, carry):
        st, sb = sht[pl.ds(l, 1), :], shb[pl.ds(l, 1), :]
        s = s_f[l + 1]
        diag = drag_s + s * total(s_f, l, st, sb)
        d_f[l] = diag
        x = v_e[l]
        image = (diag + 1.0) * x - s * total(w_f, l, st * vrt[pl.ds(l, 1), :], sb * vrb[pl.ds(l, 1), :])
        r = coef * drv_e[l] - SIGMA * image
        k_f[0, l] = r
        w = s * r
        su[0, pl.ds(l, 1), :] = w[0:1, :]
        sd[0, pl.ds(l, 1), :] = w[rows - 1:rows, :]
        return carry

    lax.fori_loop(0, levels, start_level, 0)

    def row_up(k):
        return remote(su.at[k], rb.at[k], row_ss.at[k, 0], row_rs.at[k, 0], tiles=mt - 1)

    def row_down(k):
        return remote(sd.at[k], rt.at[k], row_ss.at[k, 1], row_rs.at[k, 1], tiles=mt + 1)

    def row_start(k):
        @pl.when(mt > 0)
        def _():
            row_up(k).start()

        @pl.when(mt < T - 1)
        def _():
            row_down(k).start()

    def row_wait(k):
        @pl.when(mt < T - 1)
        def _():
            row_up(k).wait_recv()

        @pl.when(mt > 0)
        def _():
            row_down(k).wait_recv()

    def tile_sums():
        for d in range(1, T):
            a2a(d).wait_recv()
        rec[T - 1] = payload[mt]
        every = rec[...].reshape(T * cap, cells + LANES)
        hot = (every[:, cells:] == (lax.broadcasted_iota(jnp.int32, (T * cap, LANES), 1) + 1).astype(F32)).astype(F32)
        sums = lax.dot_general(hot, every[:, 0:cells], (((0,), (0,)), ((), ())),
                               precision=lax.Precision.HIGHEST, preferred_element_type=F32)
        share = cells // Q
        for q in range(Q):
            part[q] = sums[0:tpd, q * share:(q + 1) * share]
        for d in range(1, Q):
            scatter(d).start()

    def scatter(d):
        to = lax.rem(ml + d, Q)
        return remote(part.at[to], rs_rec.at[d - 1], r_ss.at[d - 1], r_rs.at[d - 1], lev=to)

    def gather(d, slot_of):
        return remote(tot_s.at[slot_of], tot_s.at[slot_of], t_ss.at[d - 1], t_rs.at[d - 1], lev=lax.rem(ml + d, Q))

    def lev_sums():
        value = part[ml]
        for d in range(1, Q):
            scatter(d).wait_recv()
            value = value + rs_rec[d - 1]
        tot_s[ml] = value
        for d in range(1, Q):
            gather(d, ml).start()

    own = slice(LANES, LANES + cols)

    def fold(x):
        return jnp.sum(x[:, own], axis=0, keepdims=True)

    for k in range(ITERS):
        row_start(k)

        def w_level(l, carry):
            w_f[l + 1] = s_f[l + 1] * k_f[k, l]
            return carry

        lax.fori_loop(0, levels, w_level, 0)
        if k == 1:
            tile_sums()
        if k == 3:
            lev_sums()
        row_wait(k)

        def step_level(l, carry):
            now, cross = carry
            s = s_f[l + 1]
            v = k_f[k, l]
            nxt = d_f[l] * v - s * total(w_f, l, rt[k, pl.ds(l, 1), :], rb[k, pl.ds(l, 1), :])
            if k + 1 < ITERS:
                k_f[k + 1, l] = nxt
                w = s * nxt
                su[k + 1, pl.ds(l, 1), :] = w[0:1, :]
                sd[k + 1, pl.ds(l, 1), :] = w[rows - 1:rows, :]
            v, nxt = v[:, own], nxt[:, own]
            return now + v * v, cross + v * nxt

        zero = jnp.zeros((rows, cols), F32)
        now, cross = lax.fori_loop(0, levels, step_level, (zero, zero))
        for j, value in ((2 * k, now), (2 * k + 1, cross)):
            line = jnp.sum(value, axis=0, keepdims=True)
            piece = line[:, 0:LANES]
            for i in range(1, cols // LANES):
                piece = piece + line[:, i * LANES:(i + 1) * LANES]
            g_send[j:j + 1, :] = piece

    def g_lev_copy(d):
        return remote(g_send, g_lev.at[d - 1], gl_ss.at[d - 1], gl_rs.at[d - 1], lev=lax.rem(ml + d, Q))

    def g_til_copy(d):
        return remote(g_mid, g_til.at[d - 1], gt_ss.at[d - 1], gt_rs.at[d - 1], tiles=lax.rem(mt + d, T))

    for d in range(1, Q):
        g_lev_copy(d).start()
    value = g_send[...]
    for d in range(1, Q):
        g_lev_copy(d).wait_recv()
        value = value + g_lev[d - 1]
    g_mid[...] = value
    for d in range(1, T):
        g_til_copy(d).start()
    for d in range(1, Q):
        gather(d, lax.rem(ml - d + Q, Q)).wait_recv()
    tot_out[...] = tot_s[...]
    for d in range(1, T):
        g_til_copy(d).wait_recv()
        value = value + g_til[d - 1]
    summed = jnp.broadcast_to(jnp.sum(value, axis=1, keepdims=True), value.shape)
    mu = [summed[j:j + 1, :] for j in range(2 * ITERS)]

    def inner(a, b):
        out = None
        for i, ai in enumerate(a):
            for j, bj in enumerate(b):
                if ai is None or bj is None:
                    continue
                term = ai * bj * mu[i + j]
                out = term if out is None else out + term
        return out

    one = jnp.ones((1, LANES), F32)
    nil = jnp.zeros((1, LANES), F32)
    res = [one]
    direc = [one]
    sol = [nil] * ITERS
    rr = mu[0]
    for it in range(ITERS):
        img = [SIGMA * ((direc[i] if i < len(direc) else nil) + (direc[i - 1] if i > 0 else nil))
               for i in range(len(direc) + 1)]
        alpha = rr / inner(direc, img)
        for i in range(len(direc)):
            sol[i] = sol[i] + alpha * direc[i]
        if it + 1 == ITERS:
            break
        res = [(res[i] if i < len(res) else nil) - alpha * img[i] for i in range(len(img))]
        new = inner(res, res)
        beta = new / rr
        direc = [res[i] + beta * (direc[i] if i < len(direc) else nil) for i in range(len(res))]
        rr = new
    wide_sol = [jnp.concatenate([jnp.broadcast_to(c, (rows, LANES))] * (cols // LANES), axis=1) for c in sol]

    def end_level(l, carry):
        x = v_e[l][:, own]
        for k in range(ITERS):
            x = x + wide_sol[k] * k_f[k, l][:, own]
        vel_out[l] = x
        return carry

    lax.fori_loop(0, levels, end_level, 0)

    @pl.when(ml < Q - 1)
    def _():
        for k in range(6):
            col_right(k).wait_send()

    @pl.when(ml > 0)
    def _():
        for k in range(6):
            col_left(k).wait_send()

    @pl.when(mt > 0)
    def _():
        v_up().wait_send()
        for k in range(ITERS):
            row_up(k).wait_send()

    @pl.when(mt < T - 1)
    def _():
        v_down().wait_send()
        for k in range(ITERS):
            row_down(k).wait_send()

    for d in range(1, T):
        a2a(d).wait_send()
        g_til_copy(d).wait_send()
    for d in range(1, Q):
        scatter(d).wait_send()
        gather(d, ml).wait_send()
        g_lev_copy(d).wait_send()


def body(T, Q, land_smb, block_weights, block_tile, block_land, block_class, ice_mask,
         thickness, prev_smb, basal_friction, driving, velocity_start):
    levels, rows, cols = velocity_start.shape
    nblk, land_cols, cells = block_weights.shape
    wide = cols + 2 * LANES
    tpd = cols * Q // LANES
    cap = max(2, 2 * nblk // T)
    cap = -(-cap // 8) * 8
    stride = -(-land_smb.shape[1] // 16) * 16
    lrows = -(-land_smb.shape[0] * stride // LANES) * LANES
    share = cells // Q
    dma = pltpu.SemaphoreType.DMA
    vm = pl.BlockSpec(memory_space=pltpu.VMEM)
    sm = pl.BlockSpec(memory_space=pltpu.SMEM)
    anyw = pl.BlockSpec(memory_space=pl.ANY)

    def f(*shape):
        return pltpu.VMEM(shape, F32)

    totals, velocity = pl.pallas_call(
        functools.partial(kernel, T, Q, cap, tpd),
        out_shape=(jax.ShapeDtypeStruct((Q, tpd, share), F32),
                   jax.ShapeDtypeStruct(velocity_start.shape, F32)),
        in_specs=[vm, anyw, sm, sm, sm] + [anyw] * 6,
        out_specs=(vm, vm),
        scratch_shapes=[
            f(levels, rows, wide), f(levels, rows, wide), f(rows, wide), f(rows, wide), f(rows, wide),
            pltpu.VMEM((rows, wide), jnp.int32),
            f(levels + 2, rows, wide), f(levels, rows, wide), f(levels + 2, rows, wide),
            f(ITERS, levels, rows, wide),
            f(2 * levels + 1, wide), f(2 * levels + 1, wide), f(2 * levels + 1, wide), f(2 * levels + 1, wide),
            f(ITERS, levels, wide), f(ITERS, levels, wide), f(ITERS, levels, wide), f(ITERS, levels, wide),
            f(levels, wide), f(levels, wide),
            f(8, LANES), f(2 * ITERS, LANES), f(Q - 1, 2 * ITERS, LANES), f(2 * ITERS, LANES),
            f(T - 1, 2 * ITERS, LANES),
            pltpu.VMEM(block_weights.shape, block_weights.dtype),
            f(lrows, LANES), pltpu.VMEM((nblk, lrows), jnp.int32), pltpu.VMEM((nblk, LANES), jnp.int32),
            f(T, cap, cells + LANES), f(T, cap, cells + LANES),
            f(Q, tpd, share), f(Q - 1, tpd, share), f(Q, tpd, share),
            dma((6,)), dma((4,)), dma((6, 2)), dma((6, 2)), dma((ITERS, 2)), dma((ITERS, 2)), dma((2,)), dma((2,)),
            dma((Q - 1,)), dma((Q - 1,)), dma((T - 1,)), dma((T - 1,)), dma((T - 1,)), dma((T - 1,)),
            dma((Q - 1,)), dma((Q - 1,)), dma((Q - 1,)), dma((Q - 1,)),
        ],
        compiler_params=pltpu.CompilerParams(collective_id=0, has_side_effects=True,
                                             vmem_limit_bytes=60 * 1024 * 1024),
        name="remap_and_solve",
    )(land_smb, block_weights, block_tile, block_land, block_class, ice_mask, thickness, prev_smb,
      basal_friction, driving, velocity_start)
    per = share // LANES
    ice_smb = totals.reshape(Q, tpd, per, LANES).transpose(0, 2, 1, 3).reshape(rows, tpd * LANES)
    return ice_smb, velocity


def solution(mesh):
    T, Q = mesh.shape["tiles"], mesh.shape["lev"]
    both = P(("tiles", "lev"))
    in_specs = (both, both, both, both, both) + (P("tiles", "lev"),) * 4 + (P(None, "tiles", "lev"),) * 2
    out_specs = (P("tiles", None), P(None, "tiles", "lev"))
    return jax.shard_map(functools.partial(body, T, Q), mesh=mesh, in_specs=in_specs,
                         out_specs=out_specs, check_vma=False)
```

```python
import functools

import jax
import jax.numpy as jnp
from jax import lax
from jax.experimental import pallas as pl
from jax.experimental.pallas import tpu as pltpu
from jax.sharding import PartitionSpec as P

ITERS = 4
VISC_FLOOR = 0.25
VERTICAL = 4.0
SMB_WEIGHT = 0.5
SIGMA = 10.0
LANES = 128
MESH = pl.DeviceIdType.MESH
F32 = jnp.float32


def kernel(
    T, Q, cap, tpd,
    land, wts, btile, bland, bclass, mask, thk, prev, fric, drv, vel,
    tot_out, vel_out,
    v_e, drv_e, thk_e, prev_e, fric_e, mask_e,
    s_f, d_f, w_f, k_f,
    vsu, vsd, vrt, vrb, su, sd, rt, rb, sht, shb,
    o_t, i_t, i_b, o_b, se_t, se_b, pe_t, pe_b, ve_t, ve_b,
    g_send, g_lev, g_mid, g_til,
    wbuf, lbuf, idx_m, tile_m, payload, rec, part, rs_rec, tot_s,
    loc_sem, w_sem, col_ss, col_rs, row_ss, row_rs, v_ss, v_rs,
    gl_ss, gl_rs, gt_ss, gt_rs, a_ss, a_rs, r_ss, r_rs, t_ss, t_rs,
):
    mt = lax.axis_index("tiles")
    ml = lax.axis_index("lev")
    levels, rows, cols = vel.shape
    wide = cols + 2 * LANES
    nblk = wts.shape[0]
    cells = wts.shape[2]
    inv_sigma = 1.0 / SIGMA

    def remote(src, dst, ss, rs, **where):
        return pltpu.make_async_remote_copy(
            src_ref=src, dst_ref=dst, send_sem=ss, recv_sem=rs,
            device_id=where, device_id_type=MESH)

    raw = (vel, drv, thk, prev, fric, mask)
    ext = (v_e, drv_e, thk_e, prev_e, fric_e, mask_e)

    def mid(ref):
        return ref.at[..., pl.ds(LANES, cols)]

    for k in range(6):
        pltpu.make_async_copy(raw[k], mid(ext[k]), loc_sem.at[k]).start()
    nchunk = w_sem.shape[0]
    per = nblk // nchunk
    for c in range(nchunk):
        pltpu.make_async_copy(wts.at[pl.ds(c * per, per)], wbuf.at[pl.ds(c * per, per)], w_sem.at[c]).start()

    bar = pltpu.get_barrier_semaphore()
    for d in range(1, Q):
        pl.semaphore_signal(bar, inc=1, device_id={"lev": lax.rem(ml + d, Q)}, device_id_type=MESH)
    for d in range(1, T):
        pl.semaphore_signal(bar, inc=1, device_id={"tiles": lax.rem(mt + d, T)}, device_id_type=MESH)

    for i in (1, T - 1):
        for j in (1, Q - 1):
            pl.semaphore_signal(bar, inc=1, device_id={"tiles": lax.rem(mt + i, T), "lev": lax.rem(ml + j, Q)},
                                device_id_type=MESH)

    s_f[0] = jnp.zeros((rows, wide), F32)
    s_f[levels + 1] = jnp.zeros((rows, wide), F32)
    w_f[0] = jnp.zeros((rows, wide), F32)
    w_f[levels + 1] = jnp.zeros((rows, wide), F32)

    @pl.when(mt == 0)
    def _():
        vrt[...] = jnp.zeros(vrt.shape, F32)
        rt[...] = jnp.zeros(rt.shape, F32)

    @pl.when(mt == T - 1)
    def _():
        vrb[...] = jnp.zeros(vrb.shape, F32)
        rb[...] = jnp.zeros(rb.shape, F32)

    for ref in ext:
        @pl.when(ml == 0)
        def _():
            ref[..., 0:LANES] = jnp.zeros(ref.shape[:-1] + (LANES,), ref.dtype)

        @pl.when(ml == Q - 1)
        def _():
            ref[..., LANES + cols:] = jnp.zeros(ref.shape[:-1] + (LANES,), ref.dtype)

    classes, lands = land.shape[0], land.shape[1]
    lbuf[...] = jnp.zeros(lbuf.shape, lbuf.dtype)
    for i in range(classes):
        lbuf[lands * i:lands * (i + 1), :] = land[i].astype(F32)
    for b in range(nblk):
        idx_m[b:b + 1, :] = jnp.full((1, idx_m.shape[1]), bclass[b] * lands + bland[b], jnp.int32)
        tile_m[b:b + 1, :] = jnp.full((1, LANES), btile[b], jnp.int32)
    pick_hot = (idx_m[...] == lax.broadcasted_iota(jnp.int32, idx_m.shape, 1)).astype(jnp.bfloat16)
    picked = jnp.dot(pick_hot, lbuf[...].astype(jnp.bfloat16), preferred_element_type=F32)
    tiles_b = tile_m[...]
    dest = tiles_b // tpd
    sub = lax.broadcasted_iota(jnp.int32, (nblk, LANES), 0)
    lane = lax.broadcasted_iota(jnp.int32, (nblk, LANES), 1)
    dest_row = jnp.sum(jnp.where(sub == lane, dest, 0), axis=0, keepdims=True)
    rank = jnp.sum(jnp.where(jnp.logical_and(dest == dest_row, lane < sub), 1.0, 0.0), axis=1, keepdims=True)
    slot = dest * cap + rank.astype(jnp.int32)
    local_id = (tiles_b % tpd + 1).astype(F32)
    nslot = T * cap
    slot_iota = lax.broadcasted_iota(jnp.int32, (nslot, LANES), 0)
    ids = jnp.zeros((nslot, LANES), F32)
    lhs = []
    for b in range(nblk):
        hit = slot_iota == slot[b:b + 1, :]
        ids = ids + jnp.where(hit, local_id[b:b + 1, :], 0.0)
        lhs.append(jnp.where(hit, picked[b:b + 1, :], 0.0).astype(jnp.bfloat16))

    def load_wait(ks):
        for k in ks:
            pltpu.make_async_copy(raw[k], mid(ext[k]), loc_sem.at[k]).wait()

    own = slice(LANES, LANES + cols)
    load_wait((0, 5))
    for l in range(levels):
        x = v_e[l, :, LANES:LANES + cols]
        vsu[l:l + 1, :] = x[0:1, :]
        vsu[levels + l:levels + l + 1, :] = x[1:2, :]
        vsd[l:l + 1, :] = x[rows - 1:rows, :]
        vsd[levels + l:levels + l + 1, :] = x[rows - 2:rows - 1, :]
    frac = mask_e[:, own].astype(F32)
    vsu[2 * levels:2 * levels + 1, :] = frac[0:1, :]
    vsd[2 * levels:2 * levels + 1, :] = frac[rows - 1:rows, :]

    pl.semaphore_wait(bar, Q - 1 + T - 1 + 4)

    def col_right(k):
        return remote(raw[k].at[..., pl.ds(cols - LANES, LANES)], ext[k].at[..., pl.ds(0, LANES)],
                      col_ss.at[k, 0], col_rs.at[k, 0], lev=ml + 1)

    def col_left(k):
        return remote(raw[k].at[..., pl.ds(0, LANES)], ext[k].at[..., pl.ds(LANES + cols, LANES)],
                      col_ss.at[k, 1], col_rs.at[k, 1], lev=ml - 1)

    @pl.when(ml < Q - 1)
    def _():
        for k in (0, 5, 1, 2, 3, 4):
            col_right(k).start()

    @pl.when(ml > 0)
    def _():
        for k in (0, 5, 1, 2, 3, 4):
            col_left(k).start()

    def col_wait(ks):
        @pl.when(ml > 0)
        def _():
            for k in ks:
                col_right(k).wait_recv()

        @pl.when(ml < Q - 1)
        def _():
            for k in ks:
                col_left(k).wait_recv()

    whole_c, low_c, high_c = pl.ds(LANES, cols), pl.ds(0, LANES), pl.ds(LANES + cols, LANES)
    first_c, last_c, every_c = pl.ds(0, LANES), pl.ds(cols - LANES, LANES), pl.ds(0, cols)
    moves = (
        (vsu, vrb, -1, 0, every_c, whole_c), (vsu, vrb, -1, -1, first_c, high_c), (vsu, vrb, -1, 1, last_c, low_c),
        (vsd, vrt, 1, 0, every_c, whole_c), (vsd, vrt, 1, -1, first_c, high_c), (vsd, vrt, 1, 1, last_c, low_c),
    )

    def there(i, j, sign):
        ok = mt > 0 if i * sign < 0 else mt < T - 1
        if j == 0:
            return ok
        return jnp.logical_and(ok, ml > 0 if j * sign < 0 else ml < Q - 1)

    def v_move(n):
        src, dst, i, j, sc, dc = moves[n]
        return remote(src.at[:, sc], dst.at[:, dc], v_ss.at[n], v_rs.at[n], tiles=mt + i, lev=ml + j)

    for n in range(6):
        @pl.when(there(moves[n][2], moves[n][3], 1))
        def _():
            v_move(n).start()

    @pl.when(ml == 0)
    def _():
        vrt[:, 0:LANES] = jnp.zeros((2 * levels + 1, LANES), F32)
        vrb[:, 0:LANES] = jnp.zeros((2 * levels + 1, LANES), F32)

    @pl.when(ml == Q - 1)
    def _():
        vrt[:, LANES + cols:] = jnp.zeros((2 * levels + 1, LANES), F32)
        vrb[:, LANES + cols:] = jnp.zeros((2 * levels + 1, LANES), F32)

    acc = jnp.zeros((nslot, cells), F32)
    for c in range(nchunk):
        pltpu.make_async_copy(wts.at[pl.ds(c * per, per)], wbuf.at[pl.ds(c * per, per)], w_sem.at[c]).wait()
        left = jnp.concatenate(lhs[c * per:(c + 1) * per], axis=1)
        right = wbuf[c * per:(c + 1) * per].reshape(per * LANES, cells)
        acc = acc + jnp.dot(left, right, preferred_element_type=F32)
    for t in range(T):
        payload[t, :, 0:cells] = acc[t * cap:(t + 1) * cap, :]
        payload[t, :, cells:] = ids[t * cap:(t + 1) * cap, :]

    def a2a(d):
        to = lax.rem(mt + d, T)
        return remote(payload.at[to], rec.at[d - 1], a_ss.at[d - 1], a_rs.at[d - 1], tiles=to)

    row_id = lax.broadcasted_iota(jnp.int32, (rows, wide), 0)

    def around(x, top, bot):
        after = jnp.where(row_id == rows - 1, bot, pltpu.roll(x, rows - 1, 0))
        before = jnp.where(row_id == 0, top, pltpu.roll(x, 1, 0))
        return before, after, pltpu.roll(x, 1, 1), pltpu.roll(x, wide - 1, 1)

    root = SIGMA ** -0.5

    def s_from(dx, dy, fr):
        q = VISC_FLOOR + 0.25 * (dx * dx) + 0.25 * (dy * dy)
        return fr * (root * jnp.exp(jnp.log(q) * (-1.0 / 6.0)))

    def across(x):
        return pltpu.roll(x, wide - 1, 1) - pltpu.roll(x, 1, 1)

    col_wait((0, 5))
    frac = mask_e[...].astype(F32)

    def s_level(l, carry):
        x = v_e[l]
        s_f[l + 1] = s_from(pltpu.roll(x, rows - 1, 0) - pltpu.roll(x, 1, 0), across(x), frac)
        o_t[pl.ds(l, 1), :] = x[0:1, :]
        i_t[pl.ds(l, 1), :] = x[1:2, :]
        i_b[pl.ds(l, 1), :] = x[rows - 2:rows - 1, :]
        o_b[pl.ds(l, 1), :] = x[rows - 1:rows, :]
        return carry

    lax.fori_loop(0, levels, s_level, 0)
    load_wait((1, 2, 3, 4))
    col_wait((1, 2, 3, 4))
    drag = frac * fric_e[...] + (1.0 - frac)
    drag_s = drag * inv_sigma - 1.0
    coef = frac * (thk_e[...] + SMB_WEIGHT * prev_e[...])

    for n in range(6):
        @pl.when(there(moves[n][2], moves[n][3], -1))
        def _():
            v_move(n).wait_recv()

    near_t, far_t = vrt[0:levels, :], vrt[levels:2 * levels, :]
    near_b, far_b = vrb[0:levels, :], vrb[levels:2 * levels, :]
    own_t, own_b = o_t[...], o_b[...]
    sht[...] = s_from(own_t - far_t, across(near_t), vrt[2 * levels:2 * levels + 1, :])
    shb[...] = s_from(far_b - own_b, across(near_b), vrb[2 * levels:2 * levels + 1, :])
    se_t[...] = s_from(i_t[...] - near_t, across(own_t), frac[0:1, :])
    se_b[...] = s_from(near_b - i_b[...], across(own_b), frac[rows - 1:rows, :])

    def with_edges(x, top, bot):
        return jnp.where(row_id == 0, top, jnp.where(row_id == rows - 1, bot, x))

    def fix_level(l, carry):
        s = with_edges(s_f[l + 1], se_t[pl.ds(l, 1), :], se_b[pl.ds(l, 1), :])
        s_f[l + 1] = s
        w_f[l + 1] = s * v_e[l]
        return carry

    lax.fori_loop(0, levels, fix_level, 0)

    def total(ref, l, top, bot):
        before, after, low, high = around(ref[l + 1], top, bot)
        return ((before + after) + (low + high)) + VERTICAL * (ref[l] + ref[l + 2])

    def inside(l):
        x = w_f[l + 1]
        after = jnp.where(row_id == rows - 1, 0.0, pltpu.roll(x, rows - 1, 0))
        before = jnp.where(row_id == 0, 0.0, pltpu.roll(x, 1, 0))
        sides = pltpu.roll(x, 1, 1) + pltpu.roll(x, wide - 1, 1)
        return ((before + after) + sides) + VERTICAL * (w_f[l] + w_f[l + 2])

    def start_level(l, carry):
        st, sb = sht[pl.ds(l, 1), :], shb[pl.ds(l, 1), :]
        s = s_f[l + 1]
        diag = drag_s + s * total(s_f, l, st, sb)
        d_f[l] = diag
        x = v_e[l]
        image = (diag + 1.0) * x - s * total(w_f, l, st * vrt[pl.ds(l, 1), :], sb * vrb[pl.ds(l, 1), :])
        r = coef * drv_e[l] - SIGMA * image
        k_f[0, l] = r
        w = s * r
        su[0, pl.ds(l, 1), :] = w[0:1, :]
        sd[0, pl.ds(l, 1), :] = w[rows - 1:rows, :]
        ve_t[pl.ds(l, 1), :] = r[0:1, :]
        ve_b[pl.ds(l, 1), :] = r[rows - 1:rows, :]
        return carry

    lax.fori_loop(0, levels, start_level, 0)

    def row_up(k):
        return remote(su.at[k], rb.at[k], row_ss.at[k, 0], row_rs.at[k, 0], tiles=mt - 1)

    def row_down(k):
        return remote(sd.at[k], rt.at[k], row_ss.at[k, 1], row_rs.at[k, 1], tiles=mt + 1)

    def row_start(k):
        if k + 1 < ITERS:
            @pl.when(mt > 0)
            def _():
                row_up(k).start()

        @pl.when(mt < T - 1)
        def _():
            row_down(k).start()

    def row_wait(k):
        if k + 1 < ITERS:
            @pl.when(mt < T - 1)
            def _():
                row_up(k).wait_recv()

        @pl.when(mt > 0)
        def _():
            row_down(k).wait_recv()

    def tile_sums():
        for d in range(1, T):
            a2a(d).wait_recv()
        rec[T - 1] = payload[mt]
        every = rec[...].reshape(T * cap, cells + LANES)
        hot = (every[:, cells:] == (lax.broadcasted_iota(jnp.int32, (T * cap, LANES), 1) + 1).astype(F32)).astype(F32)
        sums = lax.dot_general(hot, every[:, 0:cells], (((0,), (0,)), ((), ())),
                               precision=lax.Precision.HIGHEST, preferred_element_type=F32)
        share = cells // Q
        for q in range(Q):
            part[q] = sums[0:tpd, q * share:(q + 1) * share]
        for d in range(1, Q):
            scatter(d).start()

    def scatter(d):
        to = lax.rem(ml + d, Q)
        return remote(part.at[to], rs_rec.at[d - 1], r_ss.at[d - 1], r_rs.at[d - 1], lev=to)

    def gather(d, slot_of):
        return remote(tot_s.at[slot_of], tot_s.at[slot_of], t_ss.at[d - 1], t_rs.at[d - 1], lev=lax.rem(ml + d, Q))

    def lev_sums():
        value = part[ml]
        for d in range(1, Q):
            scatter(d).wait_recv()
            value = value + rs_rec[d - 1]
        tot_s[ml] = value
        for d in range(1, Q):
            gather(d, ml).start()

    def put(j, value):
        line = jnp.sum(value, axis=0, keepdims=True)
        piece = line[:, 0:LANES]
        for i in range(1, cols // LANES):
            piece = piece + line[:, i * LANES:(i + 1) * LANES]
        g_send[j:j + 1, :] = piece

    zero = jnp.zeros((rows, cols), F32)
    half = T // 2
    for k in range(ITERS):
        row_start(k)
        if k == 0:
            for d in range(1, half):
                a2a(d).start()
        if k == 1:
            for d in range(half, T):
                a2a(d).start()

        def fill_level(l, carry):
            v = k_f[k, l]
            if k > 0:
                v = with_edges(v, ve_t[pl.ds(l, 1), :], ve_b[pl.ds(l, 1), :])
                k_f[k, l] = v
            w_f[l + 1] = s_f[l + 1] * v
            mine = v[:, own]
            if k == 0:
                return carry[0] + mine * mine, carry[1]
            return carry[0] + mine * mine, carry[1] + k_f[k - 1, l][:, own] * mine

        now, cross = lax.fori_loop(0, levels, fill_level, (zero, zero))
        put(2 * k, now)
        if k > 0:
            put(2 * k - 1, cross)

        def part_level(l, carry):
            v = k_f[k, l]
            nxt = d_f[l] * v - s_f[l + 1] * inside(l)
            if k + 1 == ITERS:
                return carry + v[:, own] * nxt[:, own]
            k_f[k + 1, l] = nxt
            pe_t[pl.ds(l, 1), :] = nxt[0:1, :]
            pe_b[pl.ds(l, 1), :] = nxt[rows - 1:rows, :]
            return carry

        if k + 1 == ITERS:
            last = lax.fori_loop(0, levels, part_level, zero)
        else:
            lax.fori_loop(0, levels, part_level, 0)
        if k == 2:
            tile_sums()
        if k == 3:
            lev_sums()
        row_wait(k)
        if k + 1 < ITERS:
            top = pe_t[...] - se_t[...] * rt[k]
            bot = pe_b[...] - se_b[...] * rb[k]
            ve_t[...] = top
            ve_b[...] = bot
            su[k + 1] = se_t[...] * top
            sd[k + 1] = se_b[...] * bot
        else:
            pairs = jnp.sum(su[k][:, own] * rt[k][:, own], axis=0, keepdims=True)
            put(2 * k + 1, jnp.where(row_id[:, own] == 0, last - 2.0 * pairs, last))

    def g_lev_copy(d):
        return remote(g_send, g_lev.at[d - 1], gl_ss.at[d - 1], gl_rs.at[d - 1], lev=lax.rem(ml + d, Q))

    def g_til_copy(d):
        return remote(g_mid, g_til.at[d - 1], gt_ss.at[d - 1], gt_rs.at[d - 1], tiles=lax.rem(mt + d, T))

    for d in range(1, Q):
        g_lev_copy(d).start()
    value = g_send[...]
    for d in range(1, Q):
        g_lev_copy(d).wait_recv()
        value = value + g_lev[d - 1]
    g_mid[...] = value
    for d in range(1, T):
        g_til_copy(d).start()
    for d in range(1, Q):
        gather(d, lax.rem(ml - d + Q, Q)).wait_recv()
    share_l = tot_s.shape[2] // LANES
    for q in range(Q):
        for i in range(share_l):
            for t in range(tpd):
                tot_out[q * share_l + i:q * share_l + i + 1, t * LANES:(t + 1) * LANES] = (
                    tot_s[q, t:t + 1, i * LANES:(i + 1) * LANES])
    for d in range(1, T):
        g_til_copy(d).wait_recv()
        value = value + g_til[d - 1]
    summed = jnp.broadcast_to(jnp.sum(value, axis=1, keepdims=True), value.shape)
    mu = [summed[j:j + 1, :] for j in range(2 * ITERS)]

    def inner(a, b):
        out = None
        for i, ai in enumerate(a):
            for j, bj in enumerate(b):
                if ai is None or bj is None:
                    continue
                term = ai * bj * mu[i + j]
                out = term if out is None else out + term
        return out

    one = jnp.ones((1, LANES), F32)
    nil = jnp.zeros((1, LANES), F32)
    res = [one]
    direc = [one]
    sol = [nil] * ITERS
    rr = mu[0]
    for it in range(ITERS):
        img = [SIGMA * ((direc[i] if i < len(direc) else nil) + (direc[i - 1] if i > 0 else nil))
               for i in range(len(direc) + 1)]
        alpha = rr / inner(direc, img)
        for i in range(len(direc)):
            sol[i] = sol[i] + alpha * direc[i]
        if it + 1 == ITERS:
            break
        res = [(res[i] if i < len(res) else nil) - alpha * img[i] for i in range(len(img))]
        new = inner(res, res)
        beta = new / rr
        direc = [res[i] + beta * (direc[i] if i < len(direc) else nil) for i in range(len(res))]
        rr = new
    wide_sol = [jnp.concatenate([jnp.broadcast_to(c, (rows, LANES))] * (cols // LANES), axis=1) for c in sol]

    def end_level(l, carry):
        x = v_e[l][:, own]
        for k in range(ITERS):
            x = x + wide_sol[k] * k_f[k, l][:, own]
        vel_out[l] = x
        return carry

    lax.fori_loop(0, levels, end_level, 0)

    @pl.when(ml < Q - 1)
    def _():
        for k in range(6):
            col_right(k).wait_send()

    @pl.when(ml > 0)
    def _():
        for k in range(6):
            col_left(k).wait_send()

    for n in range(6):
        @pl.when(there(moves[n][2], moves[n][3], 1))
        def _():
            v_move(n).wait_send()

    @pl.when(mt > 0)
    def _():
        for k in range(ITERS - 1):
            row_up(k).wait_send()

    @pl.when(mt < T - 1)
    def _():
        for k in range(ITERS):
            row_down(k).wait_send()

    for d in range(1, T):
        a2a(d).wait_send()
        g_til_copy(d).wait_send()
    for d in range(1, Q):
        scatter(d).wait_send()
        gather(d, ml).wait_send()
        g_lev_copy(d).wait_send()


def body(T, Q, land_smb, block_weights, block_tile, block_land, block_class, ice_mask,
         thickness, prev_smb, basal_friction, driving, velocity_start):
    levels, rows, cols = velocity_start.shape
    nblk, land_cols, cells = block_weights.shape
    wide = cols + 2 * LANES
    tpd = cols * Q // LANES
    cap = max(2, 2 * nblk // T)
    cap = -(-cap // 8) * 8
    lrows = -(-land_smb.shape[0] * land_smb.shape[1] // LANES) * LANES
    share = cells // Q
    dma = pltpu.SemaphoreType.DMA
    vm = pl.BlockSpec(memory_space=pltpu.VMEM)
    sm = pl.BlockSpec(memory_space=pltpu.SMEM)
    anyw = pl.BlockSpec(memory_space=pl.ANY)

    def f(*shape):
        return pltpu.VMEM(shape, F32)

    return pl.pallas_call(
        functools.partial(kernel, T, Q, cap, tpd),
        out_shape=(jax.ShapeDtypeStruct((rows, tpd * LANES), F32),
                   jax.ShapeDtypeStruct(velocity_start.shape, F32)),
        in_specs=[vm, anyw, sm, sm, sm] + [anyw] * 6,
        out_specs=(vm, vm),
        scratch_shapes=[
            f(levels, rows, wide), f(levels, rows, wide), f(rows, wide), f(rows, wide), f(rows, wide),
            pltpu.VMEM((rows, wide), jnp.int32),
            f(levels + 2, rows, wide), f(levels, rows, wide), f(levels + 2, rows, wide),
            f(ITERS, levels, rows, wide),
            f(2 * levels + 1, cols), f(2 * levels + 1, cols), f(2 * levels + 1, wide), f(2 * levels + 1, wide),
            f(ITERS, levels, wide), f(ITERS, levels, wide), f(ITERS, levels, wide), f(ITERS, levels, wide),
            f(levels, wide), f(levels, wide),
            *[f(levels, wide) for _ in range(10)],
            f(2 * ITERS, LANES), f(Q - 1, 2 * ITERS, LANES), f(2 * ITERS, LANES),
            f(T - 1, 2 * ITERS, LANES),
            pltpu.VMEM(block_weights.shape, block_weights.dtype),
            f(lrows, LANES), pltpu.VMEM((nblk, lrows), jnp.int32), pltpu.VMEM((nblk, LANES), jnp.int32),
            f(T, cap, cells + LANES), f(T, cap, cells + LANES),
            f(Q, tpd, share), f(Q - 1, tpd, share), f(Q, tpd, share),
            dma((6,)), dma((4,)), dma((6, 2)), dma((6, 2)), dma((ITERS, 2)), dma((ITERS, 2)), dma((6,)), dma((6,)),
            dma((Q - 1,)), dma((Q - 1,)), dma((T - 1,)), dma((T - 1,)), dma((T - 1,)), dma((T - 1,)),
            dma((Q - 1,)), dma((Q - 1,)), dma((Q - 1,)), dma((Q - 1,)),
        ],
        compiler_params=pltpu.CompilerParams(collective_id=0, has_side_effects=True,
                                             vmem_limit_bytes=60 * 1024 * 1024),
        name="remap_and_solve",
    )(land_smb.transpose(1, 0, 2), block_weights, block_tile, block_land, block_class, ice_mask, thickness, prev_smb,
      basal_friction, driving, velocity_start)


def solution(mesh):
    T, Q = mesh.shape["tiles"], mesh.shape["lev"]
    both = P(("tiles", "lev"))
    in_specs = (both, both, both, both, both) + (P("tiles", "lev"),) * 4 + (P(None, "tiles", "lev"),) * 2
    out_specs = (P("tiles", None), P(None, "tiles", "lev"))
    return jax.shard_map(functools.partial(body, T, Q), mesh=mesh, in_specs=in_specs,
                         out_specs=out_specs, check_vma=False)
```

```python
import functools

import jax
import jax.numpy as jnp
from jax import lax
from jax.experimental import pallas as pl
from jax.experimental.pallas import tpu as pltpu
from jax.sharding import PartitionSpec as P

ITERS = 4
VISC_FLOOR = 0.25
VERTICAL = 4.0
SMB_WEIGHT = 0.5
SIGMA = 10.0
LANES = 128
MESH = pl.DeviceIdType.MESH
F32 = jnp.float32


def kernel(
    T, Q, cap, tpd,
    land, wts, btile, bland, bclass, mask, thk, prev, fric, drv, vel,
    tot_out, vel_out,
    v_e, drv_e, thk_e, prev_e, fric_e, mask_e,
    s_f, d_f, w_f, k_f,
    vsu, vsd, vrt, vrb, su, sd, rt, rb, sht, shb,
    o_t, i_t, i_b, o_b, se_t, se_b, pe_t, pe_b, ve_t, ve_b,
    g_send, g_lev, g_mid, g_til,
    wbuf, lbuf, idx_m, tile_m, payload, rec, part, rs_rec, tot_s,
    loc_sem, w_sem, col_ss, col_rs, row_ss, row_rs, v_ss, v_rs,
    gl_ss, gl_rs, gt_ss, gt_rs, a_ss, a_rs, r_ss, r_rs, t_ss, t_rs,
):
    mt = lax.axis_index("tiles")
    ml = lax.axis_index("lev")
    levels, rows, cols = vel.shape
    wide = cols + 2 * LANES
    nblk = wts.shape[0]
    cells = wts.shape[2]
    inv_sigma = 1.0 / SIGMA

    def remote(src, dst, ss, rs, **where):
        return pltpu.make_async_remote_copy(
            src_ref=src, dst_ref=dst, send_sem=ss, recv_sem=rs,
            device_id=where, device_id_type=MESH)

    raw = (vel, drv, thk, prev, fric, mask)
    ext = (v_e, drv_e, thk_e, prev_e, fric_e, mask_e)

    def mid(ref):
        return ref.at[..., pl.ds(LANES, cols)]

    for k in range(6):
        pltpu.make_async_copy(raw[k], mid(ext[k]), loc_sem.at[k]).start()
    nchunk = w_sem.shape[0]
    per = nblk // nchunk
    for c in range(nchunk):
        pltpu.make_async_copy(wts.at[pl.ds(c * per, per)], wbuf.at[pl.ds(c * per, per)], w_sem.at[c]).start()

    bar = pltpu.get_barrier_semaphore()
    for d in range(1, Q):
        pl.semaphore_signal(bar, inc=1, device_id={"lev": lax.rem(ml + d, Q)}, device_id_type=MESH)
    for d in range(1, T):
        pl.semaphore_signal(bar, inc=1, device_id={"tiles": lax.rem(mt + d, T)}, device_id_type=MESH)

    for i in (1, T - 1):
        for j in (1, Q - 1):
            pl.semaphore_signal(bar, inc=1, device_id={"tiles": lax.rem(mt + i, T), "lev": lax.rem(ml + j, Q)},
                                device_id_type=MESH)

    s_f[0] = jnp.zeros((rows, wide), F32)
    s_f[levels + 1] = jnp.zeros((rows, wide), F32)
    w_f[0] = jnp.zeros((rows, wide), F32)
    w_f[levels + 1] = jnp.zeros((rows, wide), F32)

    @pl.when(mt == 0)
    def _():
        vrt[...] = jnp.zeros(vrt.shape, F32)
        rt[...] = jnp.zeros(rt.shape, F32)

    @pl.when(mt == T - 1)
    def _():
        vrb[...] = jnp.zeros(vrb.shape, F32)
        rb[...] = jnp.zeros(rb.shape, F32)

    for ref in ext:
        @pl.when(ml == 0)
        def _():
            ref[..., 0:LANES] = jnp.zeros(ref.shape[:-1] + (LANES,), ref.dtype)

        @pl.when(ml == Q - 1)
        def _():
            ref[..., LANES + cols:] = jnp.zeros(ref.shape[:-1] + (LANES,), ref.dtype)

    classes, lands = land.shape[0], land.shape[1]
    lbuf[...] = jnp.zeros(lbuf.shape, lbuf.dtype)
    for i in range(classes):
        lbuf[lands * i:lands * (i + 1), :] = land[i].astype(F32)
    for b in range(nblk):
        idx_m[b:b + 1, :] = jnp.full((1, idx_m.shape[1]), bclass[b] * lands + bland[b], jnp.int32)
        tile_m[b:b + 1, :] = jnp.full((1, LANES), btile[b], jnp.int32)
    pick_hot = (idx_m[...] == lax.broadcasted_iota(jnp.int32, idx_m.shape, 1)).astype(jnp.bfloat16)
    picked = jnp.dot(pick_hot, lbuf[...].astype(jnp.bfloat16), preferred_element_type=F32)
    tiles_b = tile_m[...]
    dest = tiles_b // tpd
    sub = lax.broadcasted_iota(jnp.int32, (nblk, LANES), 0)
    lane = lax.broadcasted_iota(jnp.int32, (nblk, LANES), 1)
    dest_row = jnp.sum(jnp.where(sub == lane, dest, 0), axis=0, keepdims=True)
    rank = jnp.sum(jnp.where(jnp.logical_and(dest == dest_row, lane < sub), 1.0, 0.0), axis=1, keepdims=True)
    slot = dest * cap + rank.astype(jnp.int32)
    local_id = (tiles_b % tpd + 1).astype(F32)
    nslot = T * cap
    slot_iota = lax.broadcasted_iota(jnp.int32, (nslot, LANES), 0)
    ids = jnp.zeros((nslot, LANES), F32)
    lhs = []
    for b in range(nblk):
        hit = slot_iota == slot[b:b + 1, :]
        ids = ids + jnp.where(hit, local_id[b:b + 1, :], 0.0)
        lhs.append(jnp.where(hit, picked[b:b + 1, :], 0.0).astype(jnp.bfloat16))

    def load_wait(ks):
        for k in ks:
            pltpu.make_async_copy(raw[k], mid(ext[k]), loc_sem.at[k]).wait()

    own = slice(LANES, LANES + cols)
    load_wait((0, 5))
    for l in range(levels):
        x = v_e[l, :, LANES:LANES + cols]
        vsu[l:l + 1, :] = x[0:1, :]
        vsu[levels + l:levels + l + 1, :] = x[1:2, :]
        vsd[l:l + 1, :] = x[rows - 1:rows, :]
        vsd[levels + l:levels + l + 1, :] = x[rows - 2:rows - 1, :]
    frac = mask_e[:, own].astype(F32)
    vsu[2 * levels:2 * levels + 1, :] = frac[0:1, :]
    vsd[2 * levels:2 * levels + 1, :] = frac[rows - 1:rows, :]

    pl.semaphore_wait(bar, Q - 1 + T - 1 + 4)

    def col_right(k):
        return remote(raw[k].at[..., pl.ds(cols - LANES, LANES)], ext[k].at[..., pl.ds(0, LANES)],
                      col_ss.at[k, 0], col_rs.at[k, 0], lev=ml + 1)

    def col_left(k):
        return remote(raw[k].at[..., pl.ds(0, LANES)], ext[k].at[..., pl.ds(LANES + cols, LANES)],
                      col_ss.at[k, 1], col_rs.at[k, 1], lev=ml - 1)

    @pl.when(ml < Q - 1)
    def _():
        for k in (0, 5, 1, 2, 3, 4):
            col_right(k).start()

    @pl.when(ml > 0)
    def _():
        for k in (0, 5, 1, 2, 3, 4):
            col_left(k).start()

    def col_wait(ks):
        @pl.when(ml > 0)
        def _():
            for k in ks:
                col_right(k).wait_recv()

        @pl.when(ml < Q - 1)
        def _():
            for k in ks:
                col_left(k).wait_recv()

    whole_c, low_c, high_c = pl.ds(LANES, cols), pl.ds(0, LANES), pl.ds(LANES + cols, LANES)
    first_c, last_c, every_c = pl.ds(0, LANES), pl.ds(cols - LANES, LANES), pl.ds(0, cols)
    moves = (
        (vsu, vrb, -1, 0, every_c, whole_c), (vsu, vrb, -1, -1, first_c, high_c), (vsu, vrb, -1, 1, last_c, low_c),
        (vsd, vrt, 1, 0, every_c, whole_c), (vsd, vrt, 1, -1, first_c, high_c), (vsd, vrt, 1, 1, last_c, low_c),
    )

    def there(i, j, sign):
        ok = mt > 0 if i * sign < 0 else mt < T - 1
        if j == 0:
            return ok
        return jnp.logical_and(ok, ml > 0 if j * sign < 0 else ml < Q - 1)

    def v_move(n):
        src, dst, i, j, sc, dc = moves[n]
        return remote(src.at[:, sc], dst.at[:, dc], v_ss.at[n], v_rs.at[n], tiles=mt + i, lev=ml + j)

    for n in range(6):
        @pl.when(there(moves[n][2], moves[n][3], 1))
        def _():
            v_move(n).start()

    @pl.when(ml == 0)
    def _():
        vrt[:, 0:LANES] = jnp.zeros((2 * levels + 1, LANES), F32)
        vrb[:, 0:LANES] = jnp.zeros((2 * levels + 1, LANES), F32)

    @pl.when(ml == Q - 1)
    def _():
        vrt[:, LANES + cols:] = jnp.zeros((2 * levels + 1, LANES), F32)
        vrb[:, LANES + cols:] = jnp.zeros((2 * levels + 1, LANES), F32)

    acc = jnp.zeros((nslot, cells), F32)
    for c in range(nchunk):
        pltpu.make_async_copy(wts.at[pl.ds(c * per, per)], wbuf.at[pl.ds(c * per, per)], w_sem.at[c]).wait()
        left = jnp.concatenate(lhs[c * per:(c + 1) * per], axis=1)
        right = wbuf[c * per:(c + 1) * per].reshape(per * LANES, cells)
        acc = acc + jnp.dot(left, right, preferred_element_type=F32)
    for t in range(T):
        payload[t, :, 0:cells] = acc[t * cap:(t + 1) * cap, :]
        payload[t, :, cells:] = ids[t * cap:(t + 1) * cap, :]

    def a2a(d):
        to = lax.rem(mt + d, T)
        return remote(payload.at[to], rec.at[d - 1], a_ss.at[d - 1], a_rs.at[d - 1], tiles=to)

    row_id = lax.broadcasted_iota(jnp.int32, (rows, wide), 0)

    def around(x, top, bot):
        after = jnp.where(row_id == rows - 1, bot, pltpu.roll(x, rows - 1, 0))
        before = jnp.where(row_id == 0, top, pltpu.roll(x, 1, 0))
        return before, after, pltpu.roll(x, 1, 1), pltpu.roll(x, wide - 1, 1)

    root = SIGMA ** -0.5

    def s_from(dx, dy, fr):
        q = VISC_FLOOR + 0.25 * (dx * dx) + 0.25 * (dy * dy)
        return fr * (root * jnp.exp(jnp.log(q) * (-1.0 / 6.0)))

    def across(x):
        return pltpu.roll(x, wide - 1, 1) - pltpu.roll(x, 1, 1)

    col_wait((0, 5))
    frac = mask_e[...].astype(F32)

    def s_level(l, carry):
        x = v_e[l]
        s_f[l + 1] = s_from(pltpu.roll(x, rows - 1, 0) - pltpu.roll(x, 1, 0), across(x), frac)
        o_t[pl.ds(l, 1), :] = x[0:1, :]
        i_t[pl.ds(l, 1), :] = x[1:2, :]
        i_b[pl.ds(l, 1), :] = x[rows - 2:rows - 1, :]
        o_b[pl.ds(l, 1), :] = x[rows - 1:rows, :]
        return carry

    lax.fori_loop(0, levels, s_level, 0)
    load_wait((1, 2, 3, 4))
    col_wait((1, 2, 3, 4))
    drag = frac * fric_e[...] + (1.0 - frac)
    drag_s = drag * inv_sigma - 1.0
    coef = frac * (thk_e[...] + SMB_WEIGHT * prev_e[...])

    for n in range(6):
        @pl.when(there(moves[n][2], moves[n][3], -1))
        def _():
            v_move(n).wait_recv()

    near_t, far_t = vrt[0:levels, :], vrt[levels:2 * levels, :]
    near_b, far_b = vrb[0:levels, :], vrb[levels:2 * levels, :]
    own_t, own_b = o_t[...], o_b[...]
    sht[...] = s_from(own_t - far_t, across(near_t), vrt[2 * levels:2 * levels + 1, :])
    shb[...] = s_from(far_b - own_b, across(near_b), vrb[2 * levels:2 * levels + 1, :])
    se_t[...] = s_from(i_t[...] - near_t, across(own_t), frac[0:1, :])
    se_b[...] = s_from(near_b - i_b[...], across(own_b), frac[rows - 1:rows, :])

    def with_edges(x, top, bot):
        return jnp.where(row_id == 0, top, jnp.where(row_id == rows - 1, bot, x))

    def fix_level(l, carry):
        s = with_edges(s_f[l + 1], se_t[pl.ds(l, 1), :], se_b[pl.ds(l, 1), :])
        s_f[l + 1] = s
        w_f[l + 1] = s * v_e[l]
        return carry

    lax.fori_loop(0, levels, fix_level, 0)

    def total(ref, l, top, bot):
        before, after, low, high = around(ref[l + 1], top, bot)
        return ((before + after) + (low + high)) + VERTICAL * (ref[l] + ref[l + 2])

    def inside(l):
        x = w_f[l + 1]
        after = jnp.where(row_id == rows - 1, 0.0, pltpu.roll(x, rows - 1, 0))
        before = jnp.where(row_id == 0, 0.0, pltpu.roll(x, 1, 0))
        sides = pltpu.roll(x, 1, 1) + pltpu.roll(x, wide - 1, 1)
        return ((before + after) + sides) + VERTICAL * (w_f[l] + w_f[l + 2])

    def start_level(l, carry):
        st, sb = sht[pl.ds(l, 1), :], shb[pl.ds(l, 1), :]
        s = s_f[l + 1]
        diag = drag_s + s * total(s_f, l, st, sb)
        d_f[l] = diag
        x = v_e[l]
        image = (diag + 1.0) * x - s * total(w_f, l, st * vrt[pl.ds(l, 1), :], sb * vrb[pl.ds(l, 1), :])
        r = coef * drv_e[l] - SIGMA * image
        k_f[0, l] = r
        w = s * r
        su[0, pl.ds(l, 1), :] = w[0:1, :]
        sd[0, pl.ds(l, 1), :] = w[rows - 1:rows, :]
        ve_t[pl.ds(l, 1), :] = r[0:1, :]
        ve_b[pl.ds(l, 1), :] = r[rows - 1:rows, :]
        return carry

    lax.fori_loop(0, levels, start_level, 0)

    def row_up(k):
        return remote(su.at[k], rb.at[k], row_ss.at[k, 0], row_rs.at[k, 0], tiles=mt - 1)

    def row_down(k):
        return remote(sd.at[k], rt.at[k], row_ss.at[k, 1], row_rs.at[k, 1], tiles=mt + 1)

    def row_start(k):
        if k + 1 < ITERS:
            @pl.when(mt > 0)
            def _():
                row_up(k).start()

        @pl.when(mt < T - 1)
        def _():
            row_down(k).start()

    def row_wait(k):
        if k + 1 < ITERS:
            @pl.when(mt < T - 1)
            def _():
                row_up(k).wait_recv()

        @pl.when(mt > 0)
        def _():
            row_down(k).wait_recv()

    def tile_sums():
        for d in range(1, T):
            a2a(d).wait_recv()
        rec[T - 1] = payload[mt]
        every = rec[...].reshape(T * cap, cells + LANES)
        hot = (every[:, cells:] == (lax.broadcasted_iota(jnp.int32, (T * cap, LANES), 1) + 1).astype(F32)).astype(F32)
        sums = lax.dot_general(hot, every[:, 0:cells], (((0,), (0,)), ((), ())),
                               precision=lax.Precision.HIGHEST, preferred_element_type=F32)
        share = cells // Q
        for q in range(Q):
            part[q] = sums[0:tpd, q * share:(q + 1) * share]
        for d in range(1, Q):
            scatter(d).start()

    def scatter(d):
        to = lax.rem(ml + d, Q)
        return remote(part.at[to], rs_rec.at[d - 1], r_ss.at[d - 1], r_rs.at[d - 1], lev=to)

    def gather(d, slot_of):
        return remote(tot_s.at[slot_of], tot_s.at[slot_of], t_ss.at[d - 1], t_rs.at[d - 1], lev=lax.rem(ml + d, Q))

    def lev_sums():
        value = part[ml]
        for d in range(1, Q):
            scatter(d).wait_recv()
            value = value + rs_rec[d - 1]
        tot_s[ml] = value
        for d in range(1, Q):
            gather(d, ml).start()

    def put(j, value):
        line = jnp.sum(value, axis=0, keepdims=True)
        piece = line[:, 0:LANES]
        for i in range(1, cols // LANES):
            piece = piece + line[:, i * LANES:(i + 1) * LANES]
        g_send[j:j + 1, :] = piece

    zero = jnp.zeros((rows, cols), F32)
    half = T // 2
    for k in range(ITERS):
        row_start(k)
        if k == 0:
            for d in range(1, half):
                a2a(d).start()
        if k == 1:
            for d in range(half, T):
                a2a(d).start()

        def fill_level(l, carry):
            v = k_f[k, l]
            if k > 0:
                v = with_edges(v, ve_t[pl.ds(l, 1), :], ve_b[pl.ds(l, 1), :])
                k_f[k, l] = v
            w_f[l + 1] = s_f[l + 1] * v
            mine = v[:, own]
            if k == 0:
                return carry[0] + mine * mine, carry[1]
            return carry[0] + mine * mine, carry[1] + k_f[k - 1, l][:, own] * mine

        now, cross = lax.fori_loop(0, levels, fill_level, (zero, zero))
        put(2 * k, now)
        if k > 0:
            put(2 * k - 1, cross)

        def part_level(l, carry):
            v = k_f[k, l]
            nxt = d_f[l] * v - s_f[l + 1] * inside(l)
            if k + 1 == ITERS:
                return carry + v[:, own] * nxt[:, own]
            k_f[k + 1, l] = nxt
            pe_t[pl.ds(l, 1), :] = nxt[0:1, :]
            pe_b[pl.ds(l, 1), :] = nxt[rows - 1:rows, :]
            return carry

        if k + 1 == ITERS:
            last = lax.fori_loop(0, levels, part_level, zero)
        else:
            lax.fori_loop(0, levels, part_level, 0)
        if k == 2:
            tile_sums()
        if k == 3:
            lev_sums()
        row_wait(k)
        if k + 1 < ITERS:
            top = pe_t[...] - se_t[...] * rt[k]
            bot = pe_b[...] - se_b[...] * rb[k]
            ve_t[...] = top
            ve_b[...] = bot
            su[k + 1] = se_t[...] * top
            sd[k + 1] = se_b[...] * bot
        else:
            pairs = jnp.sum(su[k][:, own] * rt[k][:, own], axis=0, keepdims=True)
            put(2 * k + 1, jnp.where(row_id[:, own] == 0, last - 2.0 * pairs, last))

    def g_lev_copy(d):
        return remote(g_send, g_lev.at[d - 1], gl_ss.at[d - 1], gl_rs.at[d - 1], lev=lax.rem(ml + d, Q))

    def g_til_copy(d):
        return remote(g_mid, g_til.at[d - 1], gt_ss.at[d - 1], gt_rs.at[d - 1], tiles=lax.rem(mt + d, T))

    for d in range(1, Q):
        g_lev_copy(d).start()
    value = g_send[...]
    for d in range(1, Q):
        g_lev_copy(d).wait_recv()
        value = value + g_lev[d - 1]
    g_mid[...] = value
    for d in range(1, T):
        g_til_copy(d).start()
    for d in range(1, Q):
        gather(d, lax.rem(ml - d + Q, Q)).wait_recv()
    share_l = tot_s.shape[2] // LANES
    for q in range(Q):
        for i in range(share_l):
            for t in range(tpd):
                tot_out[q * share_l + i:q * share_l + i + 1, t * LANES:(t + 1) * LANES] = (
                    tot_s[q, t:t + 1, i * LANES:(i + 1) * LANES])
    for d in range(1, T):
        g_til_copy(d).wait_recv()
        value = value + g_til[d - 1]
    summed = jnp.broadcast_to(jnp.sum(value, axis=1, keepdims=True), value.shape)
    mu = [summed[j:j + 1, :] for j in range(2 * ITERS)]

    def inner(a, b):
        out = None
        for i, ai in enumerate(a):
            for j, bj in enumerate(b):
                if ai is None or bj is None:
                    continue
                term = ai * bj * mu[i + j]
                out = term if out is None else out + term
        return out

    one = jnp.ones((1, LANES), F32)
    nil = jnp.zeros((1, LANES), F32)
    res = [one]
    direc = [one]
    sol = [nil] * ITERS
    rr = mu[0]
    for it in range(ITERS):
        img = [SIGMA * ((direc[i] if i < len(direc) else nil) + (direc[i - 1] if i > 0 else nil))
               for i in range(len(direc) + 1)]
        alpha = rr / inner(direc, img)
        for i in range(len(direc)):
            sol[i] = sol[i] + alpha * direc[i]
        if it + 1 == ITERS:
            break
        res = [(res[i] if i < len(res) else nil) - alpha * img[i] for i in range(len(img))]
        new = inner(res, res)
        beta = new / rr
        direc = [res[i] + beta * (direc[i] if i < len(direc) else nil) for i in range(len(res))]
        rr = new
    wide_sol = [jnp.concatenate([jnp.broadcast_to(c, (rows, LANES))] * (cols // LANES), axis=1) for c in sol]

    def end_level(l, carry):
        x = v_e[l][:, own]
        for k in range(ITERS):
            x = x + wide_sol[k] * k_f[k, l][:, own]
        vel_out[l] = x
        return carry

    lax.fori_loop(0, levels, end_level, 0)

    @pl.when(ml < Q - 1)
    def _():
        for k in range(6):
            col_right(k).wait_send()

    @pl.when(ml > 0)
    def _():
        for k in range(6):
            col_left(k).wait_send()

    for n in range(6):
        @pl.when(there(moves[n][2], moves[n][3], 1))
        def _():
            v_move(n).wait_send()

    @pl.when(mt > 0)
    def _():
        for k in range(ITERS - 1):
            row_up(k).wait_send()

    @pl.when(mt < T - 1)
    def _():
        for k in range(ITERS):
            row_down(k).wait_send()

    for d in range(1, T):
        a2a(d).wait_send()
        g_til_copy(d).wait_send()
    for d in range(1, Q):
        scatter(d).wait_send()
        gather(d, ml).wait_send()
        g_lev_copy(d).wait_send()


def hand_out(smb, velocity):
    def both(a, b, a_out, b_out, sem):
        first = pltpu.make_async_copy(a, a_out, sem.at[0])
        second = pltpu.make_async_copy(b, b_out, sem.at[1])
        first.start()
        second.start()
        first.wait()
        second.wait()

    return pl.pallas_call(
        both,
        out_shape=(jax.ShapeDtypeStruct(smb.shape, F32), jax.ShapeDtypeStruct(velocity.shape, F32)),
        in_specs=[pl.BlockSpec(memory_space=pltpu.VMEM)] * 2,
        out_specs=(pl.BlockSpec(memory_space=pl.ANY),) * 2,
        scratch_shapes=[pltpu.SemaphoreType.DMA((2,))],
        name="hand_out",
    )(smb, velocity)


def body(T, Q, land_smb, block_weights, block_tile, block_land, block_class, ice_mask,
         thickness, prev_smb, basal_friction, driving, velocity_start):
    levels, rows, cols = velocity_start.shape
    nblk, land_cols, cells = block_weights.shape
    wide = cols + 2 * LANES
    tpd = cols * Q // LANES
    cap = max(2, 2 * nblk // T)
    cap = -(-cap // 8) * 8
    lrows = -(-land_smb.shape[0] * land_smb.shape[1] // LANES) * LANES
    share = cells // Q
    dma = pltpu.SemaphoreType.DMA
    vm = pl.BlockSpec(memory_space=pltpu.VMEM)
    sm = pl.BlockSpec(memory_space=pltpu.SMEM)
    anyw = pl.BlockSpec(memory_space=pl.ANY)

    def f(*shape):
        return pltpu.VMEM(shape, F32)

    totals, velocity = pl.pallas_call(
        functools.partial(kernel, T, Q, cap, tpd),
        out_shape=(jax.ShapeDtypeStruct((rows, tpd * LANES), F32),
                   jax.ShapeDtypeStruct(velocity_start.shape, F32)),
        in_specs=[vm, anyw, sm, sm, sm] + [anyw] * 6,
        out_specs=(vm, vm),
        scratch_shapes=[
            f(levels, rows, wide), f(levels, rows, wide), f(rows, wide), f(rows, wide), f(rows, wide),
            pltpu.VMEM((rows, wide), jnp.int32),
            f(levels + 2, rows, wide), f(levels, rows, wide), f(levels + 2, rows, wide),
            f(ITERS, levels, rows, wide),
            f(2 * levels + 1, cols), f(2 * levels + 1, cols), f(2 * levels + 1, wide), f(2 * levels + 1, wide),
            f(ITERS, levels, wide), f(ITERS, levels, wide), f(ITERS, levels, wide), f(ITERS, levels, wide),
            f(levels, wide), f(levels, wide),
            *[f(levels, wide) for _ in range(10)],
            f(2 * ITERS, LANES), f(Q - 1, 2 * ITERS, LANES), f(2 * ITERS, LANES),
            f(T - 1, 2 * ITERS, LANES),
            pltpu.VMEM(block_weights.shape, block_weights.dtype),
            f(lrows, LANES), pltpu.VMEM((nblk, lrows), jnp.int32), pltpu.VMEM((nblk, LANES), jnp.int32),
            f(T, cap, cells + LANES), f(T, cap, cells + LANES),
            f(Q, tpd, share), f(Q - 1, tpd, share), f(Q, tpd, share),
            dma((6,)), dma((4,)), dma((6, 2)), dma((6, 2)), dma((ITERS, 2)), dma((ITERS, 2)), dma((6,)), dma((6,)),
            dma((Q - 1,)), dma((Q - 1,)), dma((T - 1,)), dma((T - 1,)), dma((T - 1,)), dma((T - 1,)),
            dma((Q - 1,)), dma((Q - 1,)), dma((Q - 1,)), dma((Q - 1,)),
        ],
        compiler_params=pltpu.CompilerParams(collective_id=0, has_side_effects=True,
                                             vmem_limit_bytes=60 * 1024 * 1024),
        name="remap_and_solve",
    )(land_smb.transpose(1, 0, 2), block_weights, block_tile, block_land, block_class, ice_mask, thickness, prev_smb,
      basal_friction, driving, velocity_start)
    return hand_out(totals, velocity)


def solution(mesh):
    T, Q = mesh.shape["tiles"], mesh.shape["lev"]
    both = P(("tiles", "lev"))
    in_specs = (both, both, both, both, both) + (P("tiles", "lev"),) * 4 + (P(None, "tiles", "lev"),) * 2
    out_specs = (P("tiles", None), P(None, "tiles", "lev"))
    return jax.shard_map(functools.partial(body, T, Q), mesh=mesh, in_specs=in_specs,
                         out_specs=out_specs, check_vma=False)
```
